256 devices in a mesh: depth: 16 (over z, core), slab: 16 (over y, x).
Axes of the slice: x: 4, y: 4, z: 8, core: 2. Of those that a mesh axis runs over, the one named last changes fastest.
Arguments:
- state: float32 [16, 2, 2048, 2048], P('depth', None, 'slab'), may hold values from -6 to 6
- fresh: float32 [2, 2, 2048, 2048], P(None, None, 'slab'), may hold values from -6 to 6
- operators: float32 [4, 2, 2, 384, 128], replicated
- band: int32 [16], P('depth'), may hold values from 0 to 1
- freq_sched: int32 [18], replicated, may hold values from 0 to 3
Outputs:
- state_out: float32 [16, 2, 2048, 2048], P('depth', None, 'slab')
- image: float32 [16, 2048], P('depth', 'slab')
The draws below stay inside these ranges and needn't reach their ends.
All inputs are finite; a program needn't handle non-finite values.
Results may differ from the reference program's by a relative error of at most 0.00011.
Values sent between devices are 32-bit elements; how exact they have to be, the bound alone decides.
A program may use at most 128 MiB of HBM per device.

```python
import math
import jax
import jax.numpy as jnp
from jax import lax

S = 2048
R = 2048
BLK = 128
NF = 4
NB = 2
TICKS = 2
NZ = 16


def covering_ids(key, length, limit):
    values = jax.random.randint(key, (length,), 0, limit)
    order = jax.random.permutation(jax.random.fold_in(key, 7), length)
    return values.at[order[:limit]].set(jnp.arange(limit, dtype=jnp.int32)).astype(jnp.int32)


def draw_band(key, part):
    return covering_ids(jax.random.fold_in(key, 11), NZ, NB)


def draw_freq_sched(key, part):
    return covering_ids(jax.random.fold_in(key, 23), TICKS + NZ, NF)


def draw_operators(key, part):
    key_noise, key_amp, key_angle = jax.random.split(jax.random.fold_in(key, 31), 3)
    spread = 0.5
    amp = jax.random.uniform(key_amp, (NF, NB, BLK), jnp.float32, 0.6, 1.0)
    noise = jax.random.normal(key_noise, (NF, NB, 2, 3 * BLK, BLK), jnp.float32) * (spread / math.sqrt(6.0 * BLK))
    angle = jax.random.uniform(key_angle, (NF, NB, BLK), jnp.float32, -math.pi, math.pi)
    parts = jnp.stack([amp * jnp.cos(angle), amp * jnp.sin(angle)], axis=2)
    middle = parts[..., None, :] * jnp.eye(BLK, dtype=jnp.float32)
    zeros = jnp.zeros((NF, NB, 2, BLK, BLK), jnp.float32)
    return noise + jnp.concatenate([zeros, middle, zeros], axis=3)


def level_of(stream_key, extent, cuts, least, top_value):
    gain, own = 1.0, jax.random.fold_in(stream_key, 6)
    for dim, shards_of in cuts:
        heights = jnp.exp(jax.random.uniform(jax.random.fold_in(own, dim), (shards_of,), jnp.float32, least / len(cuts), top_value / len(cuts)))
        gain = gain * jnp.repeat(heights, extent[dim] // shards_of).reshape([-1 if axis == dim else 1 for axis in range(len(extent))])
    return gain


def normal_values(stream_key, extent, deviation, reach, shards=(), held_as=jnp.bfloat16):
    entries = jax.random.normal(stream_key, extent, jnp.float32) * deviation
    if len(shards) > 0:
        entries = level_of(stream_key, extent, shards, -0.22, 0.18) * entries
    return jnp.clip(entries, min=-reach, max=reach).astype(held_as)


def setup_inputs(seed: int = 0) -> dict:
    keys = jax.random.split(jax.random.key(seed), 6)
    state = normal_values(keys[0], (NZ, 2, S, R), 1.0, 6.0, ((0, 16), (2, 16)), jnp.float32)
    fresh = normal_values(keys[1], (TICKS, 2, S, R), 1.0, 6.0, ((2, 16),), jnp.float32)
    operators = draw_operators(jax.random.fold_in(keys[5], 71), 0)
    band = draw_band(jax.random.fold_in(keys[5], 71), 0)
    freq_sched = draw_freq_sched(jax.random.fold_in(keys[5], 71), 0)
    return {"state": state, "fresh": fresh, "operators": operators, "band": band, "freq_sched": freq_sched}


def cmul(triple, operator, form):
    hp = lax.Precision.HIGHEST
    real_part = jnp.einsum(form, triple[0], operator[0], precision=hp) - jnp.einsum(form, triple[1], operator[1], precision=hp)
    imag_part = jnp.einsum(form, triple[0], operator[1], precision=hp) + jnp.einsum(form, triple[1], operator[0], precision=hp)
    return jnp.stack([real_part, imag_part])


def along_middle(extended, operator):
    width = operator.shape[-1]
    count = extended.shape[1] // width - 2
    blocks = extended.reshape(2, count + 2, width, extended.shape[2])
    triple = jnp.concatenate([blocks[:, :-2], blocks[:, 1:-1], blocks[:, 2:]], axis=2)
    return cmul(triple, operator, "bic,ij->bjc").reshape(2, count * width, extended.shape[2])


def along_last(field, operator):
    width = operator.shape[-1]
    count = field.shape[2] // width
    padded = jnp.pad(field, ((0, 0), (0, 0), (width, width)))
    blocks = padded.reshape(2, field.shape[1], count + 2, width)
    triple = jnp.concatenate([blocks[:, :, :-2], blocks[:, :, 1:-1], blocks[:, :, 2:]], axis=3)
    return cmul(triple, operator, "abi,ij->abj").reshape(2, field.shape[1], count * width)


def one_step(field, operator):
    width = operator.shape[-1]
    moved = along_last(field, operator)
    padded = jnp.pad(moved, ((0, 0), (width, width), (0, 0)))
    return along_middle(padded, operator)


def reference(state, fresh, operators, band, freq_sched):
    current = state
    image = jnp.zeros((NZ, S), jnp.float32)
    owners = jnp.arange(NZ, dtype=jnp.int32)
    for tick in range(TICKS):
        freq_ids = freq_sched[(TICKS - tick + owners).astype(jnp.int32)]
        chosen = operators[freq_ids, band]
        result = lax.map(lambda pair: one_step(pair[0], pair[1]), (current, chosen))
        image = image + jnp.diagonal(result[:, 0], axis1=1, axis2=2)
        current = jnp.concatenate([fresh[tick][None], result[:-1]], axis=0)
    return current, image
```

```python
import functools

import jax
import jax.numpy as jnp
from jax import lax
from jax.experimental import pallas as pl
from jax.experimental.pallas import tpu as pltpu
from jax.sharding import PartitionSpec as P

MESH = pl.DeviceIdType.MESH
F32, BF16 = jnp.float32, jnp.bfloat16
W = 128
ND = 16
NS = 16
NP = NS // 2


def dot(a, b):
    return jnp.dot(a, b, preferred_element_type=F32)


def split(x):
    hi = x.astype(BF16)
    return hi, (x - hi.astype(F32)).astype(BF16)


def diagonal(square):
    rows = lax.broadcasted_iota(jnp.int32, (W, W), 0)
    cols = lax.broadcasted_iota(jnp.int32, (W, W), 1)
    return jnp.sum(jnp.where(rows == cols, square, 0.0), axis=0, keepdims=True)


def lanes(block, count=1):
    return pl.ds(pl.multiple_of(block * W, W), count * W)


def kernel(
    freq, band, state, fresh, operators, out, image,
    x, ops, a_hi, a_lo, b0_hi, b0_lo, b1_hi, b1_lo, wr_hi, wr_lo, ws0, ws1,
    send1, recv1, send2, recv2, obuf, tiles, y, i0, i1, r0, r1,
    in_sem, out_sem, s1_sem, r1_sem, s2_sem, r2_sem, sb_sem, rb_sem, sy_sem, ry_sem, si_sem, ri_sem,
):
    d, me = lax.axis_index("depth"), lax.axis_index("slab")
    c = lax.rem(d, 2)
    pair = me // 2
    odd = lax.rem(me, 2)
    wrap = lambda k: lax.rem(k + 2 * ND, ND)
    before, after = wrap(d - 2), wrap(d + 2)
    there1 = wrap(d + 2 * c)
    there2 = wrap(d + 2 * (1 - c))
    last = d == ND - 1
    relayed = d == 1
    at = lambda depth, slab: {"depth": depth, "slab": slab}

    ops_in = pltpu.make_async_copy(operators, ops, in_sem.at[0])
    x_in = [
        pltpu.make_async_copy(state.at[0, :, :, q * 512 : q * 512 + 512], x.at[:, :, q * 512 : q * 512 + 512], in_sem.at[1 + q])
        for q in range(4)
    ]
    ops_in.start()
    for copy in x_in:
        copy.start()

    barrier = pltpu.get_barrier_semaphore()
    signal = lambda depth, slab: pl.semaphore_signal(barrier, inc=1, device_id=at(depth, slab), device_id_type=MESH)

    @pl.loop(0, NS)
    def _(j):
        signal(before, j)

        @pl.when(j != me)
        def _():
            signal(d, j)

    signal(wrap(d - 1), me)
    signal(wrap(d + 1), me)
    signal(after, me)

    tiles[3] = jnp.full((8, W), band[0], jnp.int32)

    def operator(k, tick, tile):
        f = freq[2 - tick + k]
        pick = tiles[tile][0:1, :] > 0

        def part(component, block):
            rows = slice(block * W, block * W + W)
            return jnp.where(pick, ops[f, 1, component, rows, :], ops[f, 0, component, rows, :])

        return part

    def build_r(part):
        for block in range(3):
            re, im = part(0, block), part(1, block)
            base = block * 2 * W
            for row, left, right in ((0, re, im), (W, -im, re)):
                for col, value in ((0, left), (W, right)):
                    hi, lo = split(value)
                    wr_hi[base + row : base + row + W, col : col + W] = hi
                    wr_lo[base + row : base + row + W, col : col + W] = lo

    def build_s(part, ws):
        for block in range(3):
            re, im = part(0, block).T, part(1, block).T
            base = block * 2 * W
            for col, top, bottom in ((0, re, im), (W, -im, re)):
                for row, value in ((0, top), (W, bottom)):
                    hi, lo = split(value)
                    ws[row : row + W, base + col : base + col + W] = hi
                    ws[2 * W + row : 2 * W + row + W, base + col : base + col + W] = lo

    for ref in (a_hi, a_lo):
        ref[:, 0 : 2 * W] = jnp.zeros((W, 2 * W), BF16)
        ref[:, (NS + 1) * 2 * W :] = jnp.zeros((W, 2 * W), BF16)
    for ref in (b0_hi, b0_lo, b1_hi, b1_lo):
        ref[0 : 2 * W, 0:W] = jnp.zeros((2 * W, W), BF16)
        ref[NS * 2 * W :, W : 2 * W] = jnp.zeros((2 * W, W), BF16)

    ops_in.wait()
    build_r(operator(d, 0, 3))

    def put_a(block, re, im):
        for offset, value in ((0, re), (1, im)):
            hi, lo = split(value)
            where = lanes((block + 1) * 2 + offset)
            a_hi[:, where] = hi
            a_lo[:, where] = lo

    for q in range(4):
        x_in[q].wait()

        @pl.loop(4 * q, 4 * q + 4)
        def _(b):
            put_a(b, x[0, :, lanes(b)], x[1, :, lanes(b)])

    def along_receivers(p):
        first, second = lanes(4 * p, 6), lanes(4 * p + 2, 6)
        hi = jnp.concatenate([a_hi[:, first], a_hi[:, second]], axis=0)
        lo = jnp.concatenate([a_lo[:, first], a_lo[:, second]], axis=0)
        both = dot(jnp.concatenate([hi, lo], axis=0), wr_hi[...])
        return both[: 2 * W] + both[2 * W :] + dot(hi, wr_lo[...])

    def along_shots(p, ws, b_hi, b_lo):
        rows = pl.ds(pl.multiple_of(p * 4 * W, 4 * W), 6 * W)
        both = dot(ws[...], b_hi[rows, :])
        return both[: 2 * W] + both[2 * W :] + dot(ws[: 2 * W, :], b_lo[rows, :])

    pl.semaphore_wait(barrier, 2 * NS - 1 + 3)

    band_to = (after, wrap(d + 1), wrap(d - 1))
    band_copies = [
        pltpu.make_async_remote_copy(
            src_ref=tiles.at[3], dst_ref=tiles.at[n], send_sem=sb_sem.at[n], recv_sem=rb_sem.at[n],
            device_id=at(band_to[n], me), device_id_type=MESH,
        )
        for n in range(3)
    ]
    for copy in band_copies:
        copy.start()

    def copy1(t):
        return pltpu.make_async_remote_copy(
            src_ref=send1.at[t], dst_ref=recv1.at[me], send_sem=s1_sem.at[t], recv_sem=r1_sem.at[me],
            device_id=at(there1, t), device_id_type=MESH,
        )

    def arrival1(j):
        return pltpu.make_async_remote_copy(
            src_ref=send1.at[j], dst_ref=recv1.at[j], send_sem=s1_sem.at[j], recv_sem=r1_sem.at[j],
            device_id=at(there1, j), device_id_type=MESH,
        )

    def start1(t):
        stays = (c == 0) & (t == me)

        @pl.when(stays)
        def _():
            pltpu.make_async_copy(send1.at[t], recv1.at[me], r1_sem.at[me]).start()

        @pl.when(jnp.logical_not(stays | last))
        def _():
            copy1(t).start()

        @pl.when(last)
        def _():
            pltpu.make_async_remote_copy(
                src_ref=fresh.at[0, :, :, lanes(t)], dst_ref=recv1.at[me], send_sem=s1_sem.at[t], recv_sem=r1_sem.at[me],
                device_id=at(there1, t), device_id_type=MESH,
            ).start()

    def copy2(t):
        return pltpu.make_async_remote_copy(
            src_ref=send2.at[t], dst_ref=recv2.at[me], send_sem=s2_sem.at[t], recv_sem=r2_sem.at[me],
            device_id=at(there2, t), device_id_type=MESH,
        )

    def arrival2(j):
        return pltpu.make_async_remote_copy(
            src_ref=send2.at[j], dst_ref=recv2.at[j], send_sem=s2_sem.at[j], recv_sem=r2_sem.at[j],
            device_id=at(there2, j), device_id_type=MESH,
        )

    def start2(t):
        stays = (c == 1) & (t == me)

        @pl.when(stays)
        def _():
            pltpu.make_async_copy(send2.at[t], recv2.at[me], r2_sem.at[me]).start()

        @pl.when(jnp.logical_not(stays))
        def _():
            copy2(t).start()

    @pl.loop(0, NP)
    def _(i):
        p = lax.rem(pair - i + NP, NP)
        done = along_receivers(p)
        for n in range(2):
            for part in range(2):
                send1[2 * p + n, part] = done[n * W : n * W + W, part * W : part * W + W]
        start1(2 * p)
        start1(2 * p + 1)

    y_right = pltpu.make_async_remote_copy(
        src_ref=send1.at[jnp.minimum(me + 1, NS - 1)], dst_ref=y.at[0], send_sem=sy_sem.at[0], recv_sem=ry_sem.at[0],
        device_id=at(d, jnp.minimum(me + 1, NS - 1)), device_id_type=MESH,
    )
    y_left = pltpu.make_async_remote_copy(
        src_ref=send1.at[jnp.maximum(me - 1, 0)], dst_ref=y.at[1], send_sem=sy_sem.at[1], recv_sem=ry_sem.at[1],
        device_id=at(d, jnp.maximum(me - 1, 0)), device_id_type=MESH,
    )
    has_right, has_left = last & (me < NS - 1), last & (me > 0)
    pl.when(has_right)(y_right.start)
    pl.when(has_left)(y_left.start)

    for copy in band_copies:
        copy.wait_recv()
    swath = wrap(d - 2 * c)
    build_s(operator(swath, 0, 3 - 3 * c), ws0)
    build_s(operator(wrap(swath + 1), 1, 2 - c), ws1)
    build_r(operator(wrap(d - 1), 1, 1))

    def put_b(b_hi, b_lo, block, value):
        hi, lo = split(value)
        down = pl.ds(pl.multiple_of((block + 1) * 2 * W, 2 * W), 2 * W)
        here = pl.ds(pl.multiple_of(block * 2 * W, 2 * W), 2 * W)
        b_hi[down, 0:W] = hi
        b_hi[here, W : 2 * W] = hi
        b_lo[down, 0:W] = lo
        b_lo[here, W : 2 * W] = lo

    @pl.loop(0, NP + 4)
    def _(i):
        @pl.when(i < NP)
        def _():
            p = lax.rem(pair + i, NP)
            for n in range(2):
                arrival1(2 * p + n).wait_recv()

            def put(b_hi, b_lo):
                for n in range(2):
                    put_b(b_hi, b_lo, 2 * p + n, recv1[2 * p + n].reshape(2 * W, W))

            @pl.when(relayed)
            def _():
                put(b1_hi, b1_lo)

            @pl.when(jnp.logical_not(relayed))
            def _():
                put(b0_hi, b0_lo)

        @pl.when((i >= 2) & (i < NP + 2) & jnp.logical_not(relayed))
        def _():
            p = lax.rem(pair + 1 + i - 2, NP)
            done = along_shots(p, ws0, b0_hi, b0_lo)
            put_b(b1_hi, b1_lo, 2 * p, done[:, :W])
            put_b(b1_hi, b1_lo, 2 * p + 1, done[:, W:])

            @pl.when(p == pair)
            def _():
                square = jnp.where(odd == 0, done[:W, :W], done[:W, W:])
                i0[...] = jnp.broadcast_to(diagonal(square), (8, W))

        @pl.when(i >= 4)
        def _():
            p = lax.rem(pair + 2 + i - 4, NP)
            done = along_shots(p, ws1, b1_hi, b1_lo)
            for n in range(2):
                send2[2 * p + n] = done[:, n * W : n * W + W].reshape(2, W, W)
            start2(2 * p)
            start2(2 * p + 1)

    image0 = pltpu.make_async_remote_copy(
        src_ref=i0, dst_ref=r0, send_sem=si_sem.at[0], recv_sem=ri_sem.at[0], device_id=at(before, me), device_id_type=MESH
    )
    sends_image0 = (c == 1) & jnp.logical_not(relayed)
    pl.when(sends_image0)(image0.start)

    @pl.when(last)
    def _():
        @pl.when(me > 0)
        def _():
            y_right.wait_recv()

        @pl.when(me < NS - 1)
        def _():
            y_left.wait_recv()

        @pl.when(me == 0)
        def _():
            y[0] = jnp.zeros((2, W, W), F32)

        @pl.when(me == NS - 1)
        def _():
            y[1] = jnp.zeros((2, W, W), F32)

        part = operator(d, 0, 3)
        total = jnp.zeros((1, W), F32)
        for block, value in ((0, y[0]), (1, send1[me]), (2, y[1])):
            total += jnp.sum(value[0] * part(0, block) - value[1] * part(1, block), axis=0, keepdims=True)
        r0[...] = jnp.broadcast_to(total, (8, W))

    image1 = pltpu.make_async_remote_copy(
        src_ref=i1, dst_ref=r1, send_sem=si_sem.at[1], recv_sem=ri_sem.at[1], device_id=at(wrap(d - 1), me), device_id_type=MESH
    )

    def out_copy(p):
        return pltpu.make_async_copy(obuf.at[:, :, lanes(2 * p, 2)], out.at[0, :, :, lanes(2 * p, 2)], out_sem.at[p])

    @pl.loop(0, NP + 2)
    def _(i):
        @pl.when(i < NP)
        def _():
            p = lax.rem(pair - 2 - i + 2 * NP, NP)
            for n in range(2):
                arrival2(2 * p + n).wait_recv()
                put_a(2 * p + n, recv2[2 * p + n, 0], recv2[2 * p + n, 1])

        @pl.when(i >= 2)
        def _():
            p = lax.rem(pair - 3 - (i - 2) + 2 * NP, NP)
            done = along_receivers(p)
            for part in range(2):
                obuf[part, :, lanes(2 * p)] = done[:W, part * W : part * W + W]
                obuf[part, :, lanes(2 * p + 1)] = done[W:, part * W : part * W + W]
            out_copy(p).start()

            @pl.when(p == pair)
            def _():
                square = jnp.where(odd == 0, done[:W, :W], done[W:, :W])
                i1[...] = jnp.broadcast_to(diagonal(square), (8, W))
                image1.start()

    for copy in band_copies:
        copy.wait_send()
    pl.when(has_right)(y_right.wait_send)
    pl.when(has_left)(y_left.wait_send)

    @pl.loop(0, NS)
    def _(t):
        @pl.when(jnp.logical_not((c == 0) & (t == me)))
        def _():
            copy1(t).wait_send()

        @pl.when(jnp.logical_not((c == 1) & (t == me)))
        def _():
            copy2(t).wait_send()

    pl.when(sends_image0)(image0.wait_send)
    image1.wait_send()
    image1.wait_recv()
    pl.when((c == 1) & jnp.logical_not(last))(image0.wait_recv)

    @pl.when(c == 0)
    def _():
        image[...] = i0[0:1, :] + r1[0:1, :]

    @pl.when(c == 1)
    def _():
        image[...] = r0[0:1, :] + r1[0:1, :]

    @pl.loop(0, NP)
    def _(p):
        out_copy(p).wait()


def body(state, fresh, operators, band, freq_sched):
    any_space = pl.BlockSpec(memory_space=pl.ANY)
    smem = pl.BlockSpec(memory_space=pltpu.SMEM)
    dma, vmem = pltpu.SemaphoreType.DMA, pltpu.VMEM
    rows = state.shape[2]
    out, image = pl.pallas_call(
        kernel,
        name="relay",
        out_shape=(jax.ShapeDtypeStruct(state.shape, F32), jax.ShapeDtypeStruct((1, rows), F32)),
        in_specs=[smem, smem, any_space, any_space, any_space],
        out_specs=(any_space, pl.BlockSpec(memory_space=pltpu.VMEM)),
        scratch_shapes=[
            vmem(state.shape[1:], F32),
            vmem(operators.shape, F32),
            vmem((W, (NS + 2) * 2 * W), BF16),
            vmem((W, (NS + 2) * 2 * W), BF16),
            vmem(((NS + 1) * 2 * W, 2 * W), BF16),
            vmem(((NS + 1) * 2 * W, 2 * W), BF16),
            vmem(((NS + 1) * 2 * W, 2 * W), BF16),
            vmem(((NS + 1) * 2 * W, 2 * W), BF16),
            vmem((6 * W, 2 * W), BF16),
            vmem((6 * W, 2 * W), BF16),
            vmem((4 * W, 6 * W), BF16),
            vmem((4 * W, 6 * W), BF16),
            vmem((NS, 2, W, W), F32),
            vmem((NS, 2, W, W), F32),
            vmem((NS, 2, W, W), F32),
            vmem((NS, 2, W, W), F32),
            vmem(state.shape[1:], F32),
            vmem((4, 8, W), jnp.int32),
            vmem((2, 2, W, W), F32),
            vmem((8, W), F32),
            vmem((8, W), F32),
            vmem((8, W), F32),
            vmem((8, W), F32),
            dma((5,)),
            dma((NP,)),
            dma((NS,)),
            dma((NS,)),
            dma((NS,)),
            dma((NS,)),
            dma((3,)),
            dma((3,)),
            dma((2,)),
            dma((2,)),
            dma((2,)),
            dma((2,)),
        ],
        compiler_params=pltpu.CompilerParams(collective_id=0, has_side_effects=True, vmem_limit_bytes=56 << 20),
    )(freq_sched, band, state, fresh, operators)
    entered = lax.axis_index("depth") == 0
    return jnp.where(entered, fresh[1][None], out), image


def solution(mesh):
    return jax.shard_map(
        body,
        mesh=mesh,
        in_specs=(P("depth", None, "slab", None), P(None, None, "slab", None), P(), P("depth"), P()),
        out_specs=(P("depth", None, "slab", None), P("depth", "slab")),
        check_vma=False,
    )
```

```python
import functools

import jax
import jax.numpy as jnp
from jax import lax
from jax.experimental import pallas as pl
from jax.experimental.pallas import tpu as pltpu
from jax.sharding import PartitionSpec as P

MESH = pl.DeviceIdType.MESH
F32, BF16 = jnp.float32, jnp.bfloat16
W = 128
ND = 16
NS = 16
NP = NS // 2
CHUNKS = 4


def dot(a, b):
    return jnp.dot(a, b, preferred_element_type=F32)


def split(x):
    hi = x.astype(BF16)
    return hi, (x - hi.astype(F32)).astype(BF16)


def diagonal(square):
    rows = lax.broadcasted_iota(jnp.int32, (W, W), 0)
    cols = lax.broadcasted_iota(jnp.int32, (W, W), 1)
    return jnp.sum(jnp.where(rows == cols, square, 0.0), axis=0, keepdims=True)


def lanes(block, count=1):
    return pl.ds(pl.multiple_of(block * W, W), count * W)


def kernel(
    freq, band, state, fresh, operators, out, image,
    x, ops, a_hi, a_lo, b0_hi, b0_lo, b1_hi, b1_lo, wr_hi, wr_lo, ws0, ws1,
    send1, recv1, send2, recv2, tiles, y, i0, i1, i2, r0, r1,
    in_sem, s1_sem, r1_sem, s2_sem, r2_sem, sb_sem, rb_sem, sy_sem, ry_sem, si_sem, ri_sem,
):
    d, me = lax.axis_index("depth"), lax.axis_index("slab")
    c = lax.rem(d, 2)
    pair = me // 2
    odd = lax.rem(me, 2)
    wrap = lambda k: lax.rem(k + 2 * ND, ND)
    before, after = wrap(d - 2), wrap(d + 2)
    there1 = wrap(d + 2 * c)
    there2 = wrap(d + 2 * (1 - c))
    last = d == ND - 1
    ends = d == ND - 2
    first = d == 0
    relayed = d == 1
    at = lambda depth, slab: {"depth": depth, "slab": slab}

    ops_in = pltpu.make_async_copy(operators, ops, in_sem.at[0])
    x_in = [
        pltpu.make_async_copy(state.at[0, :, :, q * 512 : q * 512 + 512], x.at[:, :, q * 512 : q * 512 + 512], in_sem.at[1 + q])
        for q in range(4)
    ]
    for copy in x_in:
        copy.start()
    ops_in.start()

    barrier = pltpu.get_barrier_semaphore()
    signal = lambda depth, slab: pl.semaphore_signal(barrier, inc=1, device_id=at(depth, slab), device_id_type=MESH)

    @pl.loop(0, NS)
    def _(j):
        signal(before, j)

        @pl.when(j != me)
        def _():
            signal(d, j)

    signal(wrap(d - 1), me)
    signal(wrap(d + 1), me)
    signal(after, me)

    tiles[3] = jnp.full((8, W), band[0], jnp.int32)

    def operator(k, tick, tile):
        f = freq[2 - tick + k]
        pick = tiles[tile][0:1, :] > 0

        def part(component, block):
            rows = slice(block * W, block * W + W)
            return jnp.where(pick, ops[f, 1, component, rows, :], ops[f, 0, component, rows, :])

        return part

    def build_r(part):
        for block in range(3):
            re, im = part(0, block), part(1, block)
            base = block * 2 * W
            for row, left, right in ((0, re, im), (W, -im, re)):
                for col, value in ((0, left), (W, right)):
                    hi, lo = split(value)
                    wr_hi[base + row : base + row + W, col : col + W] = hi
                    wr_lo[base + row : base + row + W, col : col + W] = lo

    def build_s(part, ws):
        for block in range(3):
            re, im = part(0, block).T, part(1, block).T
            base = block * 2 * W
            for col, top, bottom in ((0, re, im), (W, -im, re)):
                for row, value in ((0, top), (W, bottom)):
                    hi, lo = split(value)
                    ws[row : row + W, base + col : base + col + W] = hi
                    ws[2 * W + row : 2 * W + row + W, base + col : base + col + W] = lo

    for ref in (a_hi, a_lo):
        ref[:, 0 : 2 * W] = jnp.zeros((W, 2 * W), BF16)
        ref[:, (NS + 1) * 2 * W :] = jnp.zeros((W, 2 * W), BF16)
    for ref in (b0_hi, b0_lo, b1_hi, b1_lo):
        ref[0 : 2 * W, 0:W] = jnp.zeros((2 * W, W), BF16)
        ref[NS * 2 * W :, W : 2 * W] = jnp.zeros((2 * W, W), BF16)

    def put_a(block, re, im):
        for offset, value in ((0, re), (1, im)):
            hi, lo = split(value)
            where = lanes((block + 1) * 2 + offset)
            a_hi[:, where] = hi
            a_lo[:, where] = lo

    for q in range(4):
        x_in[q].wait()

        @pl.loop(4 * q, 4 * q + 4)
        def _(b):
            put_a(b, x[0, :, lanes(b)], x[1, :, lanes(b)])

    ops_in.wait()
    build_r(operator(d, 0, 3))

    def along_receivers(p):
        first, second = lanes(4 * p, 6), lanes(4 * p + 2, 6)
        hi = jnp.concatenate([a_hi[:, first], a_hi[:, second]], axis=0)
        lo = jnp.concatenate([a_lo[:, first], a_lo[:, second]], axis=0)
        both = dot(jnp.concatenate([hi, lo], axis=0), wr_hi[...])
        return both[: 2 * W] + both[2 * W :] + dot(hi, wr_lo[...])

    def along_shots(p, ws, b_hi, b_lo):
        rows = pl.ds(pl.multiple_of(p * 4 * W, 4 * W), 6 * W)
        both = dot(ws[...], b_hi[rows, :])
        return both[: 2 * W] + both[2 * W :] + dot(ws[: 2 * W, :], b_lo[rows, :])

    pl.semaphore_wait(barrier, 2 * NS - 1 + 3)

    band_to = (after, wrap(d + 1), wrap(d - 1))
    band_copies = [
        pltpu.make_async_remote_copy(
            src_ref=tiles.at[3], dst_ref=tiles.at[n], send_sem=sb_sem.at[n], recv_sem=rb_sem.at[n],
            device_id=at(band_to[n], me), device_id_type=MESH,
        )
        for n in range(3)
    ]
    for copy in band_copies:
        copy.start()

    part_rows = lambda h: pl.ds(pl.multiple_of(h * (W // CHUNKS), W // CHUNKS), W // CHUNKS)

    def copy1(t):
        return pltpu.make_async_remote_copy(
            src_ref=send1.at[t], dst_ref=recv1.at[me], send_sem=s1_sem.at[t], recv_sem=r1_sem.at[me],
            device_id=at(there1, t), device_id_type=MESH,
        )

    def arrival1(j):
        return pltpu.make_async_remote_copy(
            src_ref=send1.at[j], dst_ref=recv1.at[j], send_sem=s1_sem.at[j], recv_sem=r1_sem.at[j],
            device_id=at(there1, j), device_id_type=MESH,
        )

    def start1(t, h):
        stays = (c == 0) & (t == me)
        rows, to = part_rows(h), recv1.at[me, :, part_rows(h)]

        @pl.when(stays)
        def _():
            pltpu.make_async_copy(send1.at[t, :, rows], to, r1_sem.at[me]).start()

        @pl.when(jnp.logical_not(stays | last))
        def _():
            pltpu.make_async_remote_copy(
                src_ref=send1.at[t, :, rows], dst_ref=to, send_sem=s1_sem.at[t], recv_sem=r1_sem.at[me],
                device_id=at(there1, t), device_id_type=MESH,
            ).start()

        @pl.when(last)
        def _():
            pltpu.make_async_remote_copy(
                src_ref=fresh.at[0, :, rows, lanes(t)], dst_ref=to, send_sem=s1_sem.at[t], recv_sem=r1_sem.at[me],
                device_id=at(there1, t), device_id_type=MESH,
            ).start()

    def copy2(t):
        return pltpu.make_async_remote_copy(
            src_ref=send2.at[t], dst_ref=recv2.at[me], send_sem=s2_sem.at[t], recv_sem=r2_sem.at[me],
            device_id=at(there2, t), device_id_type=MESH,
        )

    def arrival2(j):
        return pltpu.make_async_remote_copy(
            src_ref=send2.at[j], dst_ref=recv2.at[j], send_sem=s2_sem.at[j], recv_sem=r2_sem.at[j],
            device_id=at(there2, j), device_id_type=MESH,
        )

    def start2(t, h):
        stays = (c == 1) & (t == me)
        rows, to = part_rows(h), recv2.at[me, :, part_rows(h)]

        @pl.when(stays)
        def _():
            pltpu.make_async_copy(send2.at[t, :, rows], to, r2_sem.at[me]).start()

        @pl.when(jnp.logical_not(stays | ends))
        def _():
            pltpu.make_async_remote_copy(
                src_ref=send2.at[t, :, rows], dst_ref=to, send_sem=s2_sem.at[t], recv_sem=r2_sem.at[me],
                device_id=at(there2, t), device_id_type=MESH,
            ).start()

    @pl.loop(0, NP)
    def _(i):
        p = lax.rem(pair - i + NP, NP)
        done = along_receivers(p)
        for n in range(2):
            for part in range(2):
                send1[2 * p + n, part] = done[n * W : n * W + W, part * W : part * W + W]
        start1(2 * p, 0)
        start1(2 * p + 1, 0)

    @pl.loop(NP, CHUNKS * NP)
    def _(i):
        p = lax.rem(pair - i + CHUNKS * NP, NP)
        start1(2 * p, i // NP)
        start1(2 * p + 1, i // NP)

    up, down = jnp.minimum(me + 1, NS - 1), jnp.maximum(me - 1, 0)
    has_up, has_down = me < NS - 1, me > 0

    def edges(send):
        return [
            pltpu.make_async_remote_copy(
                src_ref=send.at[to], dst_ref=y.at[n], send_sem=sy_sem.at[n], recv_sem=ry_sem.at[n],
                device_id=at(d, to), device_id_type=MESH,
            )
            for n, to in ((0, up), (1, down))
        ]

    def send_edges(when, send):
        to_up, to_down = edges(send)
        pl.when(when & has_up)(to_up.start)
        pl.when(when & has_down)(to_down.start)

    def take_edges(send, part, turn):
        to_up, to_down = edges(send)
        pl.when(has_down)(to_up.wait_recv)
        pl.when(has_up)(to_down.wait_recv)
        for n, has in ((0, has_down), (1, has_up)):

            @pl.when(jnp.logical_not(has))
            def _():
                y[n] = jnp.zeros((2, W, W), F32)

        total = jnp.zeros((1, W), F32)
        for block, value in ((0, y[0]), (1, send[me]), (2, y[1])):
            re, im = turn(value[0]), turn(value[1])
            total += jnp.sum(re * part(0, block) - im * part(1, block), axis=0, keepdims=True)
        pl.when(has_up)(to_up.wait_send)
        pl.when(has_down)(to_down.wait_send)
        return jnp.broadcast_to(total, (8, W))

    send_edges(last, send1)

    for copy in band_copies:
        copy.wait_recv()
    swath = wrap(d - 2 * c)
    build_s(operator(swath, 0, 3 - 3 * c), ws0)
    build_s(operator(wrap(swath + 1), 1, 2 - c), ws1)
    build_r(operator(wrap(d - 1), 1, 1))

    def put_b(b_hi, b_lo, block, value):
        hi, lo = split(value)
        down = pl.ds(pl.multiple_of((block + 1) * 2 * W, 2 * W), 2 * W)
        here = pl.ds(pl.multiple_of(block * 2 * W, 2 * W), 2 * W)
        b_hi[down, 0:W] = hi
        b_hi[here, W : 2 * W] = hi
        b_lo[down, 0:W] = lo
        b_lo[here, W : 2 * W] = lo

    @pl.loop(0, NP + 4)
    def _(i):
        @pl.when(i < NP)
        def _():
            p = lax.rem(pair + i, NP)
            for n in range(2):
                arrival1(2 * p + n).wait_recv()

            def put(b_hi, b_lo):
                for n in range(2):
                    put_b(b_hi, b_lo, 2 * p + n, recv1[2 * p + n].reshape(2 * W, W))

            @pl.when(relayed)
            def _():
                put(b1_hi, b1_lo)

            @pl.when(jnp.logical_not(relayed))
            def _():
                put(b0_hi, b0_lo)

        @pl.when((i >= 2) & (i < NP + 2) & jnp.logical_not(relayed))
        def _():
            p = lax.rem(pair + 1 + i - 2, NP)
            done = along_shots(p, ws0, b0_hi, b0_lo)
            put_b(b1_hi, b1_lo, 2 * p, done[:, :W])
            put_b(b1_hi, b1_lo, 2 * p + 1, done[:, W:])

            @pl.when(p == pair)
            def _():
                square = jnp.where(odd == 0, done[:W, :W], done[:W, W:])
                i0[...] = jnp.broadcast_to(diagonal(square), (8, W))

        @pl.when(i >= 4)
        def _():
            p = lax.rem(pair + 2 + i - 4, NP)
            done = along_shots(p, ws1, b1_hi, b1_lo)
            for n in range(2):
                send2[2 * p + n] = done[:, n * W : n * W + W].reshape(2, W, W)
            start2(2 * p, 0)
            start2(2 * p + 1, 0)

    @pl.loop(NP, CHUNKS * NP)
    def _(i):
        p = lax.rem(pair + 2 + i, NP)
        start2(2 * p, i // NP)
        start2(2 * p + 1, i // NP)

    image0 = pltpu.make_async_remote_copy(
        src_ref=i0, dst_ref=r0, send_sem=si_sem.at[0], recv_sem=ri_sem.at[0], device_id=at(before, me), device_id_type=MESH
    )
    sends_image0 = (c == 1) & jnp.logical_not(relayed)
    pl.when(sends_image0)(image0.start)

    send_edges(ends, send2)

    @pl.when(last)
    def _():
        r0[...] = take_edges(send1, operator(d, 0, 3), lambda v: v)

    image1 = pltpu.make_async_remote_copy(
        src_ref=i1, dst_ref=r1, send_sem=si_sem.at[1], recv_sem=ri_sem.at[1], device_id=at(wrap(d - 1), me), device_id_type=MESH
    )
    image2 = pltpu.make_async_remote_copy(
        src_ref=i2, dst_ref=r1, send_sem=si_sem.at[2], recv_sem=ri_sem.at[1], device_id=at(wrap(d + 1), me), device_id_type=MESH
    )

    @pl.when(ends)
    def _():
        i2[...] = take_edges(send2, operator(wrap(d + 1), 1, 2), lambda v: v.T)
        image2.start()

    fresh_out = pltpu.make_async_copy(fresh.at[1], out.at[0], in_sem.at[5])
    pl.when(first)(fresh_out.start)

    @pl.when(jnp.logical_not(first))
    def _():
        @pl.loop(0, NP + 2)
        def _(i):
            @pl.when(i < NP)
            def _():
                p = lax.rem(pair - 2 - i + 2 * NP, NP)
                for n in range(2):
                    arrival2(2 * p + n).wait_recv()
                    put_a(2 * p + n, recv2[2 * p + n, 0], recv2[2 * p + n, 1])

            @pl.when(i >= 2)
            def _():
                p = lax.rem(pair - 3 - (i - 2) + 2 * NP, NP)
                done = along_receivers(p)
                for part in range(2):
                    out[0, part, :, lanes(2 * p)] = done[:W, part * W : part * W + W]
                    out[0, part, :, lanes(2 * p + 1)] = done[W:, part * W : part * W + W]

                @pl.when(p == pair)
                def _():
                    square = jnp.where(odd == 0, done[:W, :W], done[W:, :W])
                    i1[...] = jnp.broadcast_to(diagonal(square), (8, W))
                    image1.start()

    for copy in band_copies:
        copy.wait_send()

    @pl.loop(0, NS)
    def _(t):
        @pl.when(jnp.logical_not((c == 0) & (t == me)))
        def _():
            copy1(t).wait_send()

        @pl.when(jnp.logical_not((c == 1) & (t == me) | ends))
        def _():
            copy2(t).wait_send()

    pl.when(sends_image0)(image0.wait_send)
    pl.when(jnp.logical_not(first))(image1.wait_send)
    pl.when(ends)(image2.wait_send)
    image1.wait_recv()
    pl.when(first)(fresh_out.wait)
    pl.when((c == 1) & jnp.logical_not(last))(image0.wait_recv)

    @pl.when(c == 0)
    def _():
        image[...] = i0[0:1, :] + r1[0:1, :]

    @pl.when(c == 1)
    def _():
        image[...] = r0[0:1, :] + r1[0:1, :]


def body(state, fresh, operators, band, freq_sched):
    any_space = pl.BlockSpec(memory_space=pltpu.HBM)
    smem = pl.BlockSpec(memory_space=pltpu.SMEM)
    dma, vmem = pltpu.SemaphoreType.DMA, pltpu.VMEM
    rows = state.shape[2]
    out, image = pl.pallas_call(
        kernel,
        name="relay",
        out_shape=(jax.ShapeDtypeStruct(state.shape, F32), jax.ShapeDtypeStruct((1, rows), F32)),
        in_specs=[smem, smem, any_space, any_space, any_space],
        out_specs=(pl.BlockSpec(memory_space=pltpu.VMEM), pl.BlockSpec(memory_space=pltpu.VMEM)),
        scratch_shapes=[
            vmem(state.shape[1:], F32),
            vmem(operators.shape, F32),
            vmem((W, (NS + 2) * 2 * W), BF16),
            vmem((W, (NS + 2) * 2 * W), BF16),
            vmem(((NS + 1) * 2 * W, 2 * W), BF16),
            vmem(((NS + 1) * 2 * W, 2 * W), BF16),
            vmem(((NS + 1) * 2 * W, 2 * W), BF16),
            vmem(((NS + 1) * 2 * W, 2 * W), BF16),
            vmem((6 * W, 2 * W), BF16),
            vmem((6 * W, 2 * W), BF16),
            vmem((4 * W, 6 * W), BF16),
            vmem((4 * W, 6 * W), BF16),
            vmem((NS, 2, W, W), F32),
            vmem((NS, 2, W, W), F32),
            vmem((NS, 2, W, W), F32),
            vmem((NS, 2, W, W), F32),
            vmem((4, 8, W), jnp.int32),
            vmem((2, 2, W, W), F32),
            vmem((8, W), F32),
            vmem((8, W), F32),
            vmem((8, W), F32),
            vmem((8, W), F32),
            vmem((8, W), F32),
            dma((6,)),
            dma((NS,)),
            dma((NS,)),
            dma((NS,)),
            dma((NS,)),
            dma((3,)),
            dma((3,)),
            dma((2,)),
            dma((2,)),
            dma((3,)),
            dma((2,)),
        ],
        compiler_params=pltpu.CompilerParams(collective_id=0, has_side_effects=True, vmem_limit_bytes=36 << 20),
    )(freq_sched, band, *(pltpu.with_memory_space_constraint(v, pltpu.HBM) for v in (state, fresh, operators)))
    return out, image


def solution(mesh):
    return jax.shard_map(
        body,
        mesh=mesh,
        in_specs=(P("depth", None, "slab", None), P(None, None, "slab", None), P(), P("depth"), P()),
        out_specs=(P("depth", None, "slab", None), P("depth", "slab")),
        check_vma=False,
    )
```

```python
import functools

import jax
import jax.numpy as jnp
from jax import lax
from jax.experimental import pallas as pl
from jax.experimental.pallas import tpu as pltpu
from jax.sharding import PartitionSpec as P

MESH = pl.DeviceIdType.MESH
F32, BF16 = jnp.float32, jnp.bfloat16
W = 128
ND = 16
NS = 16
NP = NS // 2
CHUNKS = 4


def dot(a, b):
    return jnp.dot(a, b, preferred_element_type=F32)


def split(x):
    hi = x.astype(BF16)
    return hi, (x - hi.astype(F32)).astype(BF16)


def diagonal(square):
    rows = lax.broadcasted_iota(jnp.int32, (W, W), 0)
    cols = lax.broadcasted_iota(jnp.int32, (W, W), 1)
    return jnp.sum(jnp.where(rows == cols, square, 0.0), axis=0, keepdims=True)


def lanes(block, count=1):
    return pl.ds(pl.multiple_of(block * W, W), count * W)


def kernel(
    freq, band, state, fresh, operators, out, image,
    x, ops, a_hi, a_lo, b0_hi, b0_lo, b1_hi, b1_lo, wr_hi, wr_lo, ws0, ws1,
    send1, recv1, send2, recv2, tiles, y, i0, i1, i2, r0, r1,
    in_sem, s1_sem, r1_sem, s2_sem, r2_sem, sb_sem, rb_sem, sy_sem, ry_sem, si_sem, ri_sem,
):
    d, me = lax.axis_index("depth"), lax.axis_index("slab")
    c = lax.rem(d, 2)
    pair = me // 2
    odd = lax.rem(me, 2)
    wrap = lambda k: lax.rem(k + 2 * ND, ND)
    before, after = wrap(d - 2), wrap(d + 2)
    there1 = wrap(d + 2 * c)
    there2 = wrap(d + 2 * (1 - c))
    last = d == ND - 1
    ends = d == ND - 2
    first = d == 0
    relayed = d == 1
    at = lambda depth, slab: {"depth": depth, "slab": slab}

    ops_in = pltpu.make_async_copy(operators, ops, in_sem.at[0])
    x_in = [
        pltpu.make_async_copy(state.at[0, :, :, q * 512 : q * 512 + 512], x.at[:, :, q * 512 : q * 512 + 512], in_sem.at[1 + q])
        for q in range(4)
    ]
    for copy in x_in:
        copy.start()
    ops_in.start()

    barrier = pltpu.get_barrier_semaphore()
    signal = lambda depth, slab: pl.semaphore_signal(barrier, inc=1, device_id=at(depth, slab), device_id_type=MESH)

    @pl.loop(0, NS)
    def _(j):
        signal(before, j)

        @pl.when(j != me)
        def _():
            signal(d, j)

    signal(wrap(d - 1), me)
    signal(wrap(d + 1), me)
    signal(after, me)

    tiles[3] = jnp.full((8, W), band[0], jnp.int32)

    def operator(k, tick, tile):
        f = freq[2 - tick + k]
        pick = tiles[tile][0:1, :] > 0

        def part(component, block):
            rows = slice(block * W, block * W + W)
            return jnp.where(pick, ops[f, 1, component, rows, :], ops[f, 0, component, rows, :])

        return part

    def build_r(part):
        for block in range(3):
            re, im = part(0, block), part(1, block)
            base = block * 2 * W
            for row, left, right in ((0, re, im), (W, -im, re)):
                for col, value in ((0, left), (W, right)):
                    hi, lo = split(value)
                    wr_hi[base + row : base + row + W, col : col + W] = hi
                    wr_lo[base + row : base + row + W, col : col + W] = lo

    def build_s(part, ws):
        for block in range(3):
            re, im = part(0, block).T, part(1, block).T
            base = block * 2 * W
            for col, top, bottom in ((0, re, im), (W, -im, re)):
                for row, value in ((0, top), (W, bottom)):
                    hi, lo = split(value)
                    ws[row : row + W, base + col : base + col + W] = hi
                    ws[2 * W + row : 2 * W + row + W, base + col : base + col + W] = lo

    for ref in (a_hi, a_lo):
        ref[:, 0 : 2 * W] = jnp.zeros((W, 2 * W), BF16)
        ref[:, (NS + 1) * 2 * W :] = jnp.zeros((W, 2 * W), BF16)
    for ref in (b0_hi, b0_lo, b1_hi, b1_lo):
        ref[0 : 2 * W, 0:W] = jnp.zeros((2 * W, W), BF16)
        ref[NS * 2 * W :, W : 2 * W] = jnp.zeros((2 * W, W), BF16)

    def put_a(block, re, im):
        for offset, value in ((0, re), (1, im)):
            hi, lo = split(value)
            where = lanes((block + 1) * 2 + offset)
            a_hi[:, where] = hi
            a_lo[:, where] = lo

    def put_pair(p):
        for b in (2 * p, 2 * p + 1):
            put_a(b, x[0, :, lanes(b)], x[1, :, lanes(b)])

    for copy in x_in:
        copy.wait()

    @pl.loop(0, 2)
    def _(i):
        put_pair(lax.rem(pair + i, NP))

    ops_in.wait()
    build_r(operator(d, 0, 3))

    def along_receivers(p):
        first, second = lanes(4 * p, 6), lanes(4 * p + 2, 6)
        hi = jnp.concatenate([a_hi[:, first], a_hi[:, second]], axis=0)
        lo = jnp.concatenate([a_lo[:, first], a_lo[:, second]], axis=0)
        return dot(jnp.concatenate([hi, hi, lo], axis=1), jnp.concatenate([wr_hi[...], wr_lo[...], wr_hi[...]], axis=0))

    def along_shots(p, ws, b_hi, b_lo):
        rows = pl.ds(pl.multiple_of(p * 4 * W, 4 * W), 6 * W)
        hi, lo = ws[: 2 * W, :], ws[2 * W :, :]
        return dot(jnp.concatenate([hi, lo, hi], axis=1), jnp.concatenate([b_hi[rows, :], b_hi[rows, :], b_lo[rows, :]], axis=0))

    pl.semaphore_wait(barrier, 2 * NS - 1 + 3)

    band_to = (after, wrap(d + 1), wrap(d - 1))
    band_copies = [
        pltpu.make_async_remote_copy(
            src_ref=tiles.at[3], dst_ref=tiles.at[n], send_sem=sb_sem.at[n], recv_sem=rb_sem.at[n],
            device_id=at(band_to[n], me), device_id_type=MESH,
        )
        for n in range(3)
    ]
    for copy in band_copies:
        copy.start()

    part_rows = lambda h: pl.ds(pl.multiple_of(h * (W // CHUNKS), W // CHUNKS), W // CHUNKS)

    def copy1(t):
        return pltpu.make_async_remote_copy(
            src_ref=send1.at[t], dst_ref=recv1.at[me], send_sem=s1_sem.at[t], recv_sem=r1_sem.at[me],
            device_id=at(there1, t), device_id_type=MESH,
        )

    def arrival1(j):
        return pltpu.make_async_remote_copy(
            src_ref=send1.at[j], dst_ref=recv1.at[j], send_sem=s1_sem.at[j], recv_sem=r1_sem.at[j],
            device_id=at(there1, j), device_id_type=MESH,
        )

    def start1(t, h):
        stays = (c == 0) & (t == me)
        rows, to = part_rows(h), recv1.at[me, :, part_rows(h)]

        @pl.when(stays)
        def _():
            pltpu.make_async_copy(send1.at[t, :, rows], to, r1_sem.at[me]).start()

        @pl.when(jnp.logical_not(stays | last))
        def _():
            pltpu.make_async_remote_copy(
                src_ref=send1.at[t, :, rows], dst_ref=to, send_sem=s1_sem.at[t], recv_sem=r1_sem.at[me],
                device_id=at(there1, t), device_id_type=MESH,
            ).start()

        @pl.when(last)
        def _():
            pltpu.make_async_remote_copy(
                src_ref=fresh.at[0, :, rows, lanes(t)], dst_ref=to, send_sem=s1_sem.at[t], recv_sem=r1_sem.at[me],
                device_id=at(there1, t), device_id_type=MESH,
            ).start()

    def copy2(t):
        return pltpu.make_async_remote_copy(
            src_ref=send2.at[t], dst_ref=recv2.at[me], send_sem=s2_sem.at[t], recv_sem=r2_sem.at[me],
            device_id=at(there2, t), device_id_type=MESH,
        )

    def arrival2(j):
        return pltpu.make_async_remote_copy(
            src_ref=send2.at[j], dst_ref=recv2.at[j], send_sem=s2_sem.at[j], recv_sem=r2_sem.at[j],
            device_id=at(there2, j), device_id_type=MESH,
        )

    def start2(t, h):
        stays = (c == 1) & (t == me)
        rows, to = part_rows(h), recv2.at[me, :, part_rows(h)]

        @pl.when(stays)
        def _():
            pltpu.make_async_copy(send2.at[t, :, rows], to, r2_sem.at[me]).start()

        @pl.when(jnp.logical_not(stays | ends))
        def _():
            pltpu.make_async_remote_copy(
                src_ref=send2.at[t, :, rows], dst_ref=to, send_sem=s2_sem.at[t], recv_sem=r2_sem.at[me],
                device_id=at(there2, t), device_id_type=MESH,
            ).start()

    @pl.loop(0, NP)
    def _(i):
        p = lax.rem(pair - i + NP, NP)

        @pl.when(i < NP - 2)
        def _():
            put_pair(lax.rem(pair - i - 1 + NP, NP))

        done = along_receivers(p)
        for n in range(2):
            for part in range(2):
                send1[2 * p + n, part] = done[n * W : n * W + W, part * W : part * W + W]
        start1(2 * p, 0)
        start1(2 * p + 1, 0)

    @pl.loop(NP, CHUNKS * NP)
    def _(i):
        p = lax.rem(pair - i + CHUNKS * NP, NP)
        start1(2 * p, i // NP)
        start1(2 * p + 1, i // NP)

    up, down = jnp.minimum(me + 1, NS - 1), jnp.maximum(me - 1, 0)
    has_up, has_down = me < NS - 1, me > 0

    def edges(send):
        return [
            pltpu.make_async_remote_copy(
                src_ref=send.at[to], dst_ref=y.at[n], send_sem=sy_sem.at[n], recv_sem=ry_sem.at[n],
                device_id=at(d, to), device_id_type=MESH,
            )
            for n, to in ((0, up), (1, down))
        ]

    def send_edges(when, send):
        to_up, to_down = edges(send)
        pl.when(when & has_up)(to_up.start)
        pl.when(when & has_down)(to_down.start)

    def take_edges(send, part, turn):
        to_up, to_down = edges(send)
        pl.when(has_down)(to_up.wait_recv)
        pl.when(has_up)(to_down.wait_recv)
        for n, has in ((0, has_down), (1, has_up)):

            @pl.when(jnp.logical_not(has))
            def _():
                y[n] = jnp.zeros((2, W, W), F32)

        total = jnp.zeros((1, W), F32)
        for block, value in ((0, y[0]), (1, send[me]), (2, y[1])):
            re, im = turn(value[0]), turn(value[1])
            total += jnp.sum(re * part(0, block) - im * part(1, block), axis=0, keepdims=True)
        pl.when(has_up)(to_up.wait_send)
        pl.when(has_down)(to_down.wait_send)
        return jnp.broadcast_to(total, (8, W))

    send_edges(last, send1)

    for copy in band_copies:
        copy.wait_recv()
    swath = wrap(d - 2 * c)
    build_s(operator(swath, 0, 3 - 3 * c), ws0)
    build_s(operator(wrap(swath + 1), 1, 2 - c), ws1)
    build_r(operator(wrap(d - 1), 1, 1))

    def put_b(b_hi, b_lo, block, value):
        hi, lo = split(value)
        down = pl.ds(pl.multiple_of((block + 1) * 2 * W, 2 * W), 2 * W)
        here = pl.ds(pl.multiple_of(block * 2 * W, 2 * W), 2 * W)
        b_hi[down, 0:W] = hi
        b_hi[here, W : 2 * W] = hi
        b_lo[down, 0:W] = lo
        b_lo[here, W : 2 * W] = lo

    two = c == 1

    @pl.loop(0, NP + 4)
    def _(i):
        @pl.when(i < NP)
        def _():
            p = lax.rem(pair + i, NP)
            for n in range(2):
                arrival1(2 * p + n).wait_recv()

            def put(b_hi, b_lo):
                for n in range(2):
                    put_b(b_hi, b_lo, 2 * p + n, recv1[2 * p + n].reshape(2 * W, W))

            @pl.when(relayed)
            def _():
                put(b1_hi, b1_lo)

            @pl.when(jnp.logical_not(relayed))
            def _():
                put(b0_hi, b0_lo)

        @pl.when((i >= 2) & (i < NP + 2) & jnp.logical_not(relayed))
        def _():
            p = lax.rem(pair + 1 + i - 2, NP)
            done = along_shots(p, ws0, b0_hi, b0_lo)
            put_b(b1_hi, b1_lo, 2 * p, done[:, :W])
            put_b(b1_hi, b1_lo, 2 * p + 1, done[:, W:])

            @pl.when(p == pair)
            def _():
                square = jnp.where(odd == 0, done[:W, :W], done[:W, W:])
                i0[...] = jnp.broadcast_to(diagonal(square), (8, W))

        @pl.when(i >= 4)
        def _():
            p = lax.rem(pair + 2 + i - 4, NP)
            done = along_shots(p, ws1, b1_hi, b1_lo)
            for n in range(2):
                send2[2 * p + n] = done[:, n * W : n * W + W].reshape(2, W, W)
            start2(2 * p, 0)
            start2(2 * p + 1, 0)

            @pl.when(two)
            def _():
                start2(2 * p, 1)
                start2(2 * p + 1, 1)

    @pl.loop(NP, CHUNKS * NP)
    def _(i):
        @pl.when((i >= 2 * NP) | jnp.logical_not(two))
        def _():
            p = lax.rem(pair - 1 + i, NP)
            start2(2 * p, i // NP)
            start2(2 * p + 1, i // NP)

    image0 = pltpu.make_async_remote_copy(
        src_ref=i0, dst_ref=r0, send_sem=si_sem.at[0], recv_sem=ri_sem.at[0], device_id=at(before, me), device_id_type=MESH
    )
    sends_image0 = (c == 1) & jnp.logical_not(relayed)
    pl.when(sends_image0)(image0.start)

    send_edges(ends, send2)

    @pl.when(last)
    def _():
        r0[...] = take_edges(send1, operator(d, 0, 3), lambda v: v)

    image1 = pltpu.make_async_remote_copy(
        src_ref=i1, dst_ref=r1, send_sem=si_sem.at[1], recv_sem=ri_sem.at[1], device_id=at(wrap(d - 1), me), device_id_type=MESH
    )
    image2 = pltpu.make_async_remote_copy(
        src_ref=i2, dst_ref=r1, send_sem=si_sem.at[2], recv_sem=ri_sem.at[1], device_id=at(wrap(d + 1), me), device_id_type=MESH
    )

    @pl.when(ends)
    def _():
        i2[...] = take_edges(send2, operator(wrap(d + 1), 1, 2), lambda v: v.T)
        image2.start()

    fresh_out = pltpu.make_async_copy(fresh.at[1], out.at[0], in_sem.at[5])
    pl.when(first)(fresh_out.start)

    @pl.when(jnp.logical_not(first))
    def _():
        @pl.loop(0, NP + 2)
        def _(i):
            @pl.when(i < NP)
            def _():
                p = lax.rem(pair + 1 - i + NP, NP)
                for n in range(2):
                    arrival2(2 * p + n).wait_recv()
                    put_a(2 * p + n, recv2[2 * p + n, 0], recv2[2 * p + n, 1])

            @pl.when(i >= 2)
            def _():
                p = lax.rem(pair - (i - 2) + NP, NP)
                done = along_receivers(p)
                for part in range(2):
                    out[0, part, :, lanes(2 * p)] = done[:W, part * W : part * W + W]
                    out[0, part, :, lanes(2 * p + 1)] = done[W:, part * W : part * W + W]

                @pl.when(p == pair)
                def _():
                    square = jnp.where(odd == 0, done[:W, :W], done[W:, :W])
                    i1[...] = jnp.broadcast_to(diagonal(square), (8, W))
                    image1.start()

    for copy in band_copies:
        copy.wait_send()

    @pl.loop(0, NS)
    def _(t):
        @pl.when(jnp.logical_not((c == 0) & (t == me)))
        def _():
            copy1(t).wait_send()

        @pl.when(jnp.logical_not((c == 1) & (t == me) | ends))
        def _():
            copy2(t).wait_send()

    pl.when(sends_image0)(image0.wait_send)
    pl.when(jnp.logical_not(first))(image1.wait_send)
    pl.when(ends)(image2.wait_send)
    image1.wait_recv()
    pl.when(first)(fresh_out.wait)
    pl.when((c == 1) & jnp.logical_not(last))(image0.wait_recv)

    @pl.when(c == 0)
    def _():
        image[...] = i0[0:1, :] + r1[0:1, :]

    @pl.when(c == 1)
    def _():
        image[...] = r0[0:1, :] + r1[0:1, :]


def body(state, fresh, operators, band, freq_sched):
    any_space = pl.BlockSpec(memory_space=pltpu.HBM)
    smem = pl.BlockSpec(memory_space=pltpu.SMEM)
    dma, vmem = pltpu.SemaphoreType.DMA, pltpu.VMEM
    rows = state.shape[2]
    out, image = pl.pallas_call(
        kernel,
        name="relay",
        out_shape=(jax.ShapeDtypeStruct(state.shape, F32), jax.ShapeDtypeStruct((1, rows), F32)),
        in_specs=[smem, smem, any_space, any_space, any_space],
        out_specs=(pl.BlockSpec(memory_space=pltpu.VMEM), pl.BlockSpec(memory_space=pltpu.VMEM)),
        scratch_shapes=[
            vmem(state.shape[1:], F32),
            vmem(operators.shape, F32),
            vmem((W, (NS + 2) * 2 * W), BF16),
            vmem((W, (NS + 2) * 2 * W), BF16),
            vmem(((NS + 1) * 2 * W, 2 * W), BF16),
            vmem(((NS + 1) * 2 * W, 2 * W), BF16),
            vmem(((NS + 1) * 2 * W, 2 * W), BF16),
            vmem(((NS + 1) * 2 * W, 2 * W), BF16),
            vmem((6 * W, 2 * W), BF16),
            vmem((6 * W, 2 * W), BF16),
            vmem((4 * W, 6 * W), BF16),
            vmem((4 * W, 6 * W), BF16),
            vmem((NS, 2, W, W), F32),
            vmem((NS, 2, W, W), F32),
            vmem((NS, 2, W, W), F32),
            vmem((NS, 2, W, W), F32),
            vmem((4, 8, W), jnp.int32),
            vmem((2, 2, W, W), F32),
            vmem((8, W), F32),
            vmem((8, W), F32),
            vmem((8, W), F32),
            vmem((8, W), F32),
            vmem((8, W), F32),
            dma((6,)),
            dma((NS,)),
            dma((NS,)),
            dma((NS,)),
            dma((NS,)),
            dma((3,)),
            dma((3,)),
            dma((2,)),
            dma((2,)),
            dma((3,)),
            dma((2,)),
        ],
        compiler_params=pltpu.CompilerParams(collective_id=0, has_side_effects=True, vmem_limit_bytes=36 << 20),
    )(freq_sched, band, *(pltpu.with_memory_space_constraint(v, pltpu.HBM) for v in (state, fresh, operators)))
    return out, image


def solution(mesh):
    return jax.shard_map(
        body,
        mesh=mesh,
        in_specs=(P("depth", None, "slab", None), P(None, None, "slab", None), P(), P("depth"), P()),
        out_specs=(P("depth", None, "slab", None), P("depth", "slab")),
        check_vma=False,
    )
```

```python
import functools

import jax
import jax.numpy as jnp
from jax import lax
from jax.experimental import pallas as pl
from jax.experimental.pallas import tpu as pltpu
from jax.sharding import PartitionSpec as P

MESH = pl.DeviceIdType.MESH
F32, BF16 = jnp.float32, jnp.bfloat16
W = 128
ND = 16
NS = 16
NP = NS // 2
CHUNKS = 4


def dot(a, b):
    return jnp.dot(a, b, preferred_element_type=F32)


def split(x):
    hi = x.astype(BF16)
    return hi, (x - hi.astype(F32)).astype(BF16)


def diagonal(square):
    rows = lax.broadcasted_iota(jnp.int32, (W, W), 0)
    cols = lax.broadcasted_iota(jnp.int32, (W, W), 1)
    return jnp.sum(jnp.where(rows == cols, square, 0.0), axis=0, keepdims=True)


def lanes(block, count=1):
    return pl.ds(pl.multiple_of(block * W, W), count * W)


def kernel(
    freq, band, state, fresh, operators, out, image,
    x, ops, a_hi, a_lo, b0_hi, b0_lo, b1_hi, b1_lo, wr_hi, wr_lo, ws0, ws1,
    send1, recv1, send2, recv2, tiles, y, i0, i1, i2, r0, r1,
    in_sem, s1_sem, r1_sem, s2_sem, r2_sem, sb_sem, rb_sem, sy_sem, ry_sem, si_sem, ri_sem,
):
    d, me = lax.axis_index("depth"), lax.axis_index("slab")
    c = lax.rem(d, 2)
    pair = me // 2
    odd = lax.rem(me, 2)
    wrap = lambda k: lax.rem(k + 2 * ND, ND)
    before, after = wrap(d - 2), wrap(d + 2)
    there1 = wrap(d + 2 * c)
    there2 = wrap(d + 2 * (1 - c))
    last = d == ND - 1
    ends = d == ND - 2
    first = d == 0
    relayed = d == 1
    at = lambda depth, slab: {"depth": depth, "slab": slab}

    ops_in = pltpu.make_async_copy(operators, ops, in_sem.at[0])
    x_in = [
        pltpu.make_async_copy(state.at[0, :, :, q * 512 : q * 512 + 512], x.at[:, :, q * 512 : q * 512 + 512], in_sem.at[1 + q])
        for q in range(4)
    ]
    for copy in x_in:
        copy.start()
    ops_in.start()

    barrier = pltpu.get_barrier_semaphore()
    signal = lambda depth, slab: pl.semaphore_signal(barrier, inc=1, device_id=at(depth, slab), device_id_type=MESH)

    @pl.loop(0, NS)
    def _(j):
        signal(before, j)

        @pl.when(j != me)
        def _():
            signal(d, j)

    signal(wrap(d - 1), me)
    signal(wrap(d + 1), me)
    signal(after, me)

    tiles[3] = jnp.full((8, W), band[0], jnp.int32)

    def operator(k, tick, tile):
        f = freq[2 - tick + k]
        pick = tiles[tile][0:1, :] > 0

        def part(component, block):
            rows = slice(block * W, block * W + W)
            return jnp.where(pick, ops[f, 1, component, rows, :], ops[f, 0, component, rows, :])

        return part

    def build_r(part):
        for block in range(3):
            re, im = part(0, block), part(1, block)
            base = block * 2 * W
            for row, left, right in ((0, re, im), (W, -im, re)):
                for col, value in ((0, left), (W, right)):
                    hi, lo = split(value)
                    wr_hi[base + row : base + row + W, col : col + W] = hi
                    wr_lo[base + row : base + row + W, col : col + W] = lo

    def build_s(part, ws):
        for block in range(3):
            re, im = part(0, block).T, part(1, block).T
            base = block * 2 * W
            for col, top, bottom in ((0, re, im), (W, -im, re)):
                for row, value in ((0, top), (W, bottom)):
                    hi, lo = split(value)
                    ws[row : row + W, base + col : base + col + W] = hi
                    ws[2 * W + row : 2 * W + row + W, base + col : base + col + W] = lo

    for ref in (a_hi, a_lo):
        ref[:, 0 : 2 * W] = jnp.zeros((W, 2 * W), BF16)
        ref[:, (NS + 1) * 2 * W :] = jnp.zeros((W, 2 * W), BF16)
    for ref in (b0_hi, b0_lo, b1_hi, b1_lo):
        ref[0 : 2 * W, 0:W] = jnp.zeros((2 * W, W), BF16)
        ref[NS * 2 * W :, W : 2 * W] = jnp.zeros((2 * W, W), BF16)

    def put_a(block, re, im):
        for offset, value in ((0, re), (1, im)):
            hi, lo = split(value)
            where = lanes((block + 1) * 2 + offset)
            a_hi[:, where] = hi
            a_lo[:, where] = lo

    def put_pair(p):
        for b in (2 * p, 2 * p + 1):
            put_a(b, x[0, :, lanes(b)], x[1, :, lanes(b)])

    for copy in x_in:
        copy.wait()

    @pl.loop(0, 2)
    def _(i):
        put_pair(lax.rem(pair + i, NP))

    ops_in.wait()
    build_r(operator(d, 0, 3))

    def along_receivers(p):
        first, second = lanes(4 * p, 6), lanes(4 * p + 2, 6)
        hi = jnp.concatenate([a_hi[:, first], a_hi[:, second]], axis=0)
        lo = jnp.concatenate([a_lo[:, first], a_lo[:, second]], axis=0)
        return dot(jnp.concatenate([hi, hi, lo], axis=1), jnp.concatenate([wr_hi[...], wr_lo[...], wr_hi[...]], axis=0))

    def along_shots(p, ws, b_hi, b_lo):
        rows = pl.ds(pl.multiple_of(p * 4 * W, 4 * W), 6 * W)
        hi, lo = ws[: 2 * W, :], ws[2 * W :, :]
        return dot(jnp.concatenate([hi, lo, hi], axis=1), jnp.concatenate([b_hi[rows, :], b_hi[rows, :], b_lo[rows, :]], axis=0))

    pl.semaphore_wait(barrier, 2 * NS - 1 + 3)

    band_to = (after, wrap(d + 1), wrap(d - 1))
    band_copies = [
        pltpu.make_async_remote_copy(
            src_ref=tiles.at[3], dst_ref=tiles.at[n], send_sem=sb_sem.at[n], recv_sem=rb_sem.at[n],
            device_id=at(band_to[n], me), device_id_type=MESH,
        )
        for n in range(3)
    ]
    for copy in band_copies:
        copy.start()

    part_rows = lambda h: pl.ds(pl.multiple_of(h * (W // CHUNKS), W // CHUNKS), W // CHUNKS)

    def copy1(t):
        return pltpu.make_async_remote_copy(
            src_ref=send1.at[t], dst_ref=recv1.at[me], send_sem=s1_sem.at[t], recv_sem=r1_sem.at[me],
            device_id=at(there1, t), device_id_type=MESH,
        )

    def arrival1(j):
        return pltpu.make_async_remote_copy(
            src_ref=send1.at[j], dst_ref=recv1.at[j], send_sem=s1_sem.at[j], recv_sem=r1_sem.at[j],
            device_id=at(there1, j), device_id_type=MESH,
        )

    def start1(t, h):
        stays = (c == 0) & (t == me)
        rows, to = part_rows(h), recv1.at[me, :, part_rows(h)]

        @pl.when(stays)
        def _():
            pltpu.make_async_copy(send1.at[t, :, rows], to, r1_sem.at[me]).start()

        @pl.when(jnp.logical_not(stays | last))
        def _():
            pltpu.make_async_remote_copy(
                src_ref=send1.at[t, :, rows], dst_ref=to, send_sem=s1_sem.at[t], recv_sem=r1_sem.at[me],
                device_id=at(there1, t), device_id_type=MESH,
            ).start()

        @pl.when(last)
        def _():
            pltpu.make_async_remote_copy(
                src_ref=fresh.at[0, :, rows, lanes(t)], dst_ref=to, send_sem=s1_sem.at[t], recv_sem=r1_sem.at[me],
                device_id=at(there1, t), device_id_type=MESH,
            ).start()

    def copy2(t):
        return pltpu.make_async_remote_copy(
            src_ref=send2.at[t], dst_ref=recv2.at[me], send_sem=s2_sem.at[t], recv_sem=r2_sem.at[me],
            device_id=at(there2, t), device_id_type=MESH,
        )

    def arrival2(j):
        return pltpu.make_async_remote_copy(
            src_ref=send2.at[j], dst_ref=recv2.at[j], send_sem=s2_sem.at[j], recv_sem=r2_sem.at[j],
            device_id=at(there2, j), device_id_type=MESH,
        )

    def start2(t, h):
        stays = (c == 1) & (t == me)
        rows, to = part_rows(h), recv2.at[me, :, part_rows(h)]

        @pl.when(stays)
        def _():
            pltpu.make_async_copy(send2.at[t, :, rows], to, r2_sem.at[me]).start()

        @pl.when(jnp.logical_not(stays | ends))
        def _():
            pltpu.make_async_remote_copy(
                src_ref=send2.at[t, :, rows], dst_ref=to, send_sem=s2_sem.at[t], recv_sem=r2_sem.at[me],
                device_id=at(there2, t), device_id_type=MESH,
            ).start()

    @pl.loop(0, NP)
    def _(i):
        p = lax.rem(pair - i + NP, NP)

        @pl.when(i < NP - 2)
        def _():
            put_pair(lax.rem(pair - i - 1 + NP, NP))

        done = along_receivers(p)
        for n in range(2):
            for part in range(2):
                send1[2 * p + n, part] = done[n * W : n * W + W, part * W : part * W + W]
        start1(2 * p, 0)
        start1(2 * p + 1, 0)

    @pl.loop(NP, CHUNKS * NP)
    def _(i):
        p = lax.rem(pair - i + CHUNKS * NP, NP)
        start1(2 * p, i // NP)
        start1(2 * p + 1, i // NP)

    up, down = jnp.minimum(me + 1, NS - 1), jnp.maximum(me - 1, 0)
    has_up, has_down = me < NS - 1, me > 0

    def edges(send):
        return [
            pltpu.make_async_remote_copy(
                src_ref=send.at[to], dst_ref=y.at[n], send_sem=sy_sem.at[n], recv_sem=ry_sem.at[n],
                device_id=at(d, to), device_id_type=MESH,
            )
            for n, to in ((0, up), (1, down))
        ]

    def send_edges(when, send):
        to_up, to_down = edges(send)
        pl.when(when & has_up)(to_up.start)
        pl.when(when & has_down)(to_down.start)

    def take_edges(send, part, turn):
        to_up, to_down = edges(send)
        pl.when(has_down)(to_up.wait_recv)
        pl.when(has_up)(to_down.wait_recv)
        for n, has in ((0, has_down), (1, has_up)):

            @pl.when(jnp.logical_not(has))
            def _():
                y[n] = jnp.zeros((2, W, W), F32)

        total = jnp.zeros((1, W), F32)
        for block, value in ((0, y[0]), (1, send[me]), (2, y[1])):
            re, im = turn(value[0]), turn(value[1])
            total += jnp.sum(re * part(0, block) - im * part(1, block), axis=0, keepdims=True)
        pl.when(has_up)(to_up.wait_send)
        pl.when(has_down)(to_down.wait_send)
        return jnp.broadcast_to(total, (8, W))

    send_edges(last, send1)

    for copy in band_copies:
        copy.wait_recv()
    swath = wrap(d - 2 * c)
    build_s(operator(swath, 0, 3 - 3 * c), ws0)
    build_s(operator(wrap(swath + 1), 1, 2 - c), ws1)
    build_r(operator(wrap(d - 1), 1, 1))

    def put_b(b_hi, b_lo, block, value):
        hi, lo = split(value)
        down = pl.ds(pl.multiple_of((block + 1) * 2 * W, 2 * W), 2 * W)
        here = pl.ds(pl.multiple_of(block * 2 * W, 2 * W), 2 * W)
        b_hi[down, 0:W] = hi
        b_hi[here, W : 2 * W] = hi
        b_lo[down, 0:W] = lo
        b_lo[here, W : 2 * W] = lo

    two = (d != 7) & (d != 9)

    @pl.loop(0, NP + 4)
    def _(i):
        @pl.when(i < NP)
        def _():
            p = lax.rem(pair + i, NP)
            for n in range(2):
                arrival1(2 * p + n).wait_recv()

            def put(b_hi, b_lo):
                for n in range(2):
                    put_b(b_hi, b_lo, 2 * p + n, recv1[2 * p + n].reshape(2 * W, W))

            @pl.when(relayed)
            def _():
                put(b1_hi, b1_lo)

            @pl.when(jnp.logical_not(relayed))
            def _():
                put(b0_hi, b0_lo)

        @pl.when((i >= 2) & (i < NP + 2) & jnp.logical_not(relayed))
        def _():
            p = lax.rem(pair + 1 + i - 2, NP)
            done = along_shots(p, ws0, b0_hi, b0_lo)
            put_b(b1_hi, b1_lo, 2 * p, done[:, :W])
            put_b(b1_hi, b1_lo, 2 * p + 1, done[:, W:])

            @pl.when(p == pair)
            def _():
                square = jnp.where(odd == 0, done[:W, :W], done[:W, W:])
                i0[...] = jnp.broadcast_to(diagonal(square), (8, W))

        @pl.when(i >= 4)
        def _():
            p = lax.rem(pair + 2 + i - 4, NP)
            done = along_shots(p, ws1, b1_hi, b1_lo)
            for n in range(2):
                send2[2 * p + n] = done[:, n * W : n * W + W].reshape(2, W, W)
            start2(2 * p, 0)
            start2(2 * p + 1, 0)

            @pl.when(two)
            def _():
                start2(2 * p, 1)
                start2(2 * p + 1, 1)

    @pl.loop(NP, CHUNKS * NP)
    def _(i):
        @pl.when((i >= 2 * NP) | jnp.logical_not(two))
        def _():
            p = lax.rem(pair - 1 + i, NP)
            start2(2 * p, i // NP)
            start2(2 * p + 1, i // NP)

    image0 = pltpu.make_async_remote_copy(
        src_ref=i0, dst_ref=r0, send_sem=si_sem.at[0], recv_sem=ri_sem.at[0], device_id=at(before, me), device_id_type=MESH
    )
    sends_image0 = (c == 1) & jnp.logical_not(relayed)
    pl.when(sends_image0)(image0.start)

    send_edges(ends, send2)

    @pl.when(last)
    def _():
        r0[...] = take_edges(send1, operator(d, 0, 3), lambda v: v)

    image1 = pltpu.make_async_remote_copy(
        src_ref=i1, dst_ref=r1, send_sem=si_sem.at[1], recv_sem=ri_sem.at[1], device_id=at(wrap(d - 1), me), device_id_type=MESH
    )
    image2 = pltpu.make_async_remote_copy(
        src_ref=i2, dst_ref=r1, send_sem=si_sem.at[2], recv_sem=ri_sem.at[1], device_id=at(wrap(d + 1), me), device_id_type=MESH
    )

    @pl.when(ends)
    def _():
        i2[...] = take_edges(send2, operator(wrap(d + 1), 1, 2), lambda v: v.T)
        image2.start()

    fresh_out = pltpu.make_async_copy(fresh.at[1], out.at[0], in_sem.at[5])
    pl.when(first)(fresh_out.start)

    @pl.when(jnp.logical_not(first))
    def _():
        @pl.loop(0, NP + 2)
        def _(i):
            @pl.when(i < NP)
            def _():
                p = lax.rem(pair + 1 - i + NP, NP)
                for n in range(2):
                    arrival2(2 * p + n).wait_recv()
                    put_a(2 * p + n, recv2[2 * p + n, 0], recv2[2 * p + n, 1])

            @pl.when(i >= 2)
            def _():
                p = lax.rem(pair - (i - 2) + NP, NP)
                done = along_receivers(p)
                for part in range(2):
                    out[0, part, :, lanes(2 * p)] = done[:W, part * W : part * W + W]
                    out[0, part, :, lanes(2 * p + 1)] = done[W:, part * W : part * W + W]

                @pl.when(p == pair)
                def _():
                    square = jnp.where(odd == 0, done[:W, :W], done[W:, :W])
                    i1[...] = jnp.broadcast_to(diagonal(square), (8, W))
                    image1.start()

    for copy in band_copies:
        copy.wait_send()

    @pl.loop(0, NS)
    def _(t):
        @pl.when(jnp.logical_not((c == 0) & (t == me)))
        def _():
            copy1(t).wait_send()

        @pl.when(jnp.logical_not((c == 1) & (t == me) | ends))
        def _():
            copy2(t).wait_send()

    pl.when(sends_image0)(image0.wait_send)
    pl.when(jnp.logical_not(first))(image1.wait_send)
    pl.when(ends)(image2.wait_send)
    image1.wait_recv()
    pl.when(first)(fresh_out.wait)
    pl.when((c == 1) & jnp.logical_not(last))(image0.wait_recv)

    @pl.when(c == 0)
    def _():
        image[...] = i0[0:1, :] + r1[0:1, :]

    @pl.when(c == 1)
    def _():
        image[...] = r0[0:1, :] + r1[0:1, :]


def body(state, fresh, operators, band, freq_sched):
    any_space = pl.BlockSpec(memory_space=pltpu.HBM)
    smem = pl.BlockSpec(memory_space=pltpu.SMEM)
    dma, vmem = pltpu.SemaphoreType.DMA, pltpu.VMEM
    rows = state.shape[2]
    out, image = pl.pallas_call(
        kernel,
        name="relay",
        out_shape=(jax.ShapeDtypeStruct(state.shape, F32), jax.ShapeDtypeStruct((1, rows), F32)),
        in_specs=[smem, smem, any_space, any_space, any_space],
        out_specs=(pl.BlockSpec(memory_space=pltpu.VMEM), pl.BlockSpec(memory_space=pltpu.VMEM)),
        scratch_shapes=[
            vmem(state.shape[1:], F32),
            vmem(operators.shape, F32),
            vmem((W, (NS + 2) * 2 * W), BF16),
            vmem((W, (NS + 2) * 2 * W), BF16),
            vmem(((NS + 1) * 2 * W, 2 * W), BF16),
            vmem(((NS + 1) * 2 * W, 2 * W), BF16),
            vmem(((NS + 1) * 2 * W, 2 * W), BF16),
            vmem(((NS + 1) * 2 * W, 2 * W), BF16),
            vmem((6 * W, 2 * W), BF16),
            vmem((6 * W, 2 * W), BF16),
            vmem((4 * W, 6 * W), BF16),
            vmem((4 * W, 6 * W), BF16),
            vmem((NS, 2, W, W), F32),
            vmem((NS, 2, W, W), F32),
            vmem((NS, 2, W, W), F32),
            vmem((NS, 2, W, W), F32),
            vmem((4, 8, W), jnp.int32),
            vmem((2, 2, W, W), F32),
            vmem((8, W), F32),
            vmem((8, W), F32),
            vmem((8, W), F32),
            vmem((8, W), F32),
            vmem((8, W), F32),
            dma((6,)),
            dma((NS,)),
            dma((NS,)),
            dma((NS,)),
            dma((NS,)),
            dma((3,)),
            dma((3,)),
            dma((2,)),
            dma((2,)),
            dma((3,)),
            dma((2,)),
        ],
        compiler_params=pltpu.CompilerParams(collective_id=0, has_side_effects=True, vmem_limit_bytes=36 << 20),
    )(freq_sched, band, *(pltpu.with_memory_space_constraint(v, pltpu.HBM) for v in (state, fresh, operators)))
    return out, image


def solution(mesh):
    return jax.shard_map(
        body,
        mesh=mesh,
        in_specs=(P("depth", None, "slab", None), P(None, None, "slab", None), P(), P("depth"), P()),
        out_specs=(P("depth", None, "slab", None), P("depth", "slab")),
        check_vma=False,
    )
```
